32 devices in a mesh: clips: 2 (over y), ctx: 4 (over z), head: 4 (over x, core).
Axes of the slice: x: 2, y: 2, z: 4, core: 2. Of those that a mesh axis runs over, the one named last changes fastest.
Arguments:
- queries: bfloat16 [9216, 1536], P(('clips', 'ctx', 'head')), parts along dimension 0
- keys: bfloat16 [9216, 1536], P(('clips', 'ctx', 'head')), parts along dimension 0
- values: bfloat16 [9216, 1536], P(('clips', 'ctx', 'head')), parts along dimension 0, may hold values from -4.5 to 4.5
- neighbors: int32 [24, 8], P(('clips', 'ctx')), parts along dimension 0, may hold values from 0 to 11, as said below
- tile_counts: int32 [24], P(('clips', 'ctx')), parts along dimension 0, may hold values from 192 to 384
Outputs:
- attended: bfloat16 [9216, 1536], P(('clips', 'ctx', 'head')), parts along dimension 0
The draws below stay inside these ranges and needn't reach their ends.
There are 2 independent parts, one for each index of `clips`. The reference program is written for one: setup_inputs(seed, part) draws one part's arguments, and reference() takes and returns one part's arrays. A program takes and returns all parts, laid end to end along the dimension named above; each array names one. Nothing has to cross between parts.
Inputs may be any that keep to these rules, and one draw needn't show every extreme that they name: `neighbors`: row t starts with t itself, followed by 8 - 1 distinct other tiles of t's 3 x 3 x 3 window of tiles: frame layer, row and column each differ from t's by at most one.
All inputs are finite; a program needn't handle non-finite values.
Results may differ from the reference program's by a relative error of at most 0.0049.
Values may be sent and summed in bfloat16 or wider, within the bound.
A program may use at most 64 MiB of HBM per device.

```python
import jax
import jax.numpy as jnp
from jax import lax

HEADS = 12
DH = 128
TILE = 384
TH = 2
TW = 3
NB = 8
NT = 12
TOKENS = 4608


def base_field(key):
    return jax.random.truncated_normal(key, -4.5, 4.5, (TOKENS, HEADS * DH), jnp.float32)


def draw_keys(key, part):
    field = base_field(jax.random.fold_in(key, 7))
    return field.astype(jnp.bfloat16)


def draw_queries(key, part):
    field = base_field(jax.random.fold_in(key, 9))
    return field.astype(jnp.bfloat16)


def draw_neighbors(key, part):
    layer_size = TH * TW
    layers = NT // layer_size
    tile_ids = jnp.arange(NT, dtype=jnp.int32)
    frame = tile_ids // layer_size
    row_pos = tile_ids // TW % TH
    col_pos = tile_ids % TW
    cube = jnp.concatenate([jnp.arange(13, dtype=jnp.int32), jnp.arange(14, 27, dtype=jnp.int32)])
    step_frame = cube // 9 - 1
    step_row = cube // 3 % 3 - 1
    step_col = cube % 3 - 1
    cand_frame = frame[:, None] + step_frame[None, :]
    cand_row = row_pos[:, None] + step_row[None, :]
    cand_col = col_pos[:, None] + step_col[None, :]
    in_range = (cand_frame >= 0) & (cand_frame < layers) & (cand_row >= 0) & (cand_row < TH) & (cand_col >= 0) & (cand_col < TW)
    candidates = cand_frame * layer_size + cand_row * TW + cand_col
    priority = jax.vmap(lambda sub_key: jax.random.permutation(sub_key, 26))(jax.random.split(jax.random.fold_in(key, 5), NT))
    priority = priority + jnp.where(in_range, 0, 1000)
    ranking = jnp.argsort(priority, axis=1, stable=True)
    chosen = jnp.take_along_axis(candidates, ranking, axis=1)[:, :NB - 1]
    return jnp.concatenate([tile_ids[:, None], chosen], axis=1).astype(jnp.int32)


def draw_tile_counts(key, part):
    ragged = jax.random.randint(jax.random.fold_in(key, 1), (NT,), 0, 4) == 0
    shorter = jax.random.randint(jax.random.fold_in(key, 2), (NT,), TILE // 2, TILE)
    counts_all = jnp.where(ragged, shorter, TILE)
    counts_all = counts_all.at[0].set(TILE).at[1].set(TILE // 2)
    return counts_all.astype(jnp.int32)


def level_of(stream_key, shape, shards, least, top_value):
    def one(position, shards_of):
        draws = jax.random.uniform(jax.random.fold_in(jax.random.fold_in(stream_key, 6), position), (shards_of,), jnp.float32, least / len(shards), top_value / len(shards))
        return jnp.repeat(jnp.exp(draws), shape[position] // shards_of).reshape((-1,) + (1,) * (len(shape) - position - 1))

    loudness = one(*shards[0])
    for cut in shards[1:]:
        loudness = loudness * one(*cut)
    return loudness


def noise(stream_key, dims, scale, reach, cuts=(), held_as=jnp.bfloat16):
    values = jax.random.normal(stream_key, dims, jnp.float32) * scale
    if len(cuts) > 0:
        values = level_of(stream_key, dims, cuts, -0.22, 0.18) * values
    return jnp.clip(values, min=-reach, max=reach).astype(held_as)


def setup_inputs(seed: int = 0, part: int = 0) -> dict:
    splits = jax.random.split(jax.random.key(seed), 6)
    part_keys = jax.random.split(jax.random.fold_in(splits[5], part), 6)
    return {
        "queries": draw_queries(jax.random.fold_in(jax.random.fold_in(splits[5], part), 71), part),
        "keys": draw_keys(jax.random.fold_in(jax.random.fold_in(splits[5], part), 71), part),
        "values": noise(part_keys[2], (TOKENS, HEADS * DH), 1.0, 4.5, ((0, 16),)),
        "neighbors": draw_neighbors(jax.random.fold_in(jax.random.fold_in(splits[5], part), 71), part),
        "tile_counts": draw_tile_counts(jax.random.fold_in(jax.random.fold_in(splits[5], part), 71), part),
    }


def attend_tile(query_tile, key_rows, value_rows, key_mask):
    scores = jnp.einsum("qhd,khd->hqk", query_tile.astype(jnp.float32), key_rows.astype(jnp.float32)) * (DH ** -0.5)
    scores = jnp.where(key_mask[None, None, :], scores, -jnp.inf)
    highest = jnp.max(scores, axis=2, keepdims=True)
    weights = jnp.exp(scores - highest)
    totals = jnp.sum(weights, axis=2, keepdims=True)
    rounded = lax.optimization_barrier(weights.astype(jnp.bfloat16))
    summed = jnp.einsum("hqk,khd->qhd", rounded.astype(jnp.float32), value_rows.astype(jnp.float32))
    return (summed / jnp.transpose(totals, (1, 0, 2))).astype(jnp.bfloat16)


def reference(queries, keys, values, neighbors, tile_counts):
    query_tiles = queries.reshape(NT, TILE, HEADS, DH)
    key_tiles = keys.reshape(NT, TILE, HEADS, DH)
    value_tiles = values.reshape(NT, TILE, HEADS, DH)
    slot_index = jnp.arange(TILE, dtype=jnp.int32)

    def one_tile(tile_id):
        listed = neighbors[tile_id]
        listed_live = listed >= 0
        safe_ids = jnp.maximum(listed, 0).astype(jnp.int32)
        key_rows = key_tiles[safe_ids].reshape(NB * TILE, HEADS, DH)
        value_rows = value_tiles[safe_ids].reshape(NB * TILE, HEADS, DH)
        key_mask = (listed_live[:, None] & (slot_index[None, :] < tile_counts[safe_ids][:, None])).reshape(NB * TILE)
        return attend_tile(query_tiles[tile_id], key_rows, value_rows, key_mask)

    result = lax.map(one_tile, jnp.arange(NT, dtype=jnp.int32))
    return result.reshape(TOKENS, HEADS * DH)
```

```python
import jax
import jax.numpy as jnp
from jax import lax
from jax.sharding import PartitionSpec as P
from jax.experimental import pallas as pl
from jax.experimental.pallas import tpu as pltpu

DH = 128
TILE = 384
NB = 8
REACH = 10
HOPS = 4


def shifted(array, axis, by):
    peers = lax.axis_size(axis)
    pairs = [(i, i + by) for i in range(peers) if 0 <= i + by < peers]
    return lax.ppermute(array, axis, pairs)


def join_pieces(pieces):
    return tuple(
        (jnp.concatenate([piece[member] for piece in pieces], axis=0) for member in range(3))
    )


def attend_kernel(lists_ref, counts_ref, query_ref, *refs):
    key_refs = refs[:NB]
    value_refs = refs[NB : 2 * NB]
    out_ref = refs[2 * NB]
    tile = pl.program_id(0)
    query_rows = query_ref[...]
    slot_index = lax.broadcasted_iota(jnp.int32, (TILE, TILE), 1)
    scores = []
    for entry in range(NB):
        part = lax.dot_general(
            query_rows, key_refs[entry][...], (((1,), (1,)), ((), ())),
            preferred_element_type=jnp.float32,
        ) * DH ** (-0.5)
        live = slot_index < counts_ref[lists_ref[tile, entry]]
        scores.append(jnp.where(live, part, -jnp.inf))
    highest = scores[0].max(axis=1, keepdims=True)
    for part in scores[1:]:
        highest = jnp.maximum(highest, part.max(axis=1, keepdims=True))
    totals = jnp.zeros((TILE, 1), jnp.float32)
    summed = jnp.zeros((TILE, DH), jnp.float32)
    for entry in range(NB):
        weights = jnp.exp(scores[entry] - highest)
        totals = totals + weights.sum(axis=1, keepdims=True)
        summed = summed + jnp.dot(
            weights.astype(jnp.bfloat16), value_refs[entry][...],
            preferred_element_type=jnp.float32,
        )
    out_ref[...] = (summed / totals).astype(out_ref.dtype)


def attend(local_lists, ext_counts, query_tiles, ext_keys, ext_values):
    tiles_here, _, local_width = query_tiles.shape
    local_heads = local_width // DH
    own = pl.BlockSpec((None, TILE, DH), lambda t, h, lists, counts: (t, 0, h))

    def listed(entry):
        return pl.BlockSpec(
            (None, TILE, DH), lambda t, h, lists, counts: (lists[t, entry], 0, h)
        )

    spec = pltpu.PrefetchScalarGridSpec(
        num_scalar_prefetch=2,
        grid=(tiles_here, local_heads),
        in_specs=[own] + [listed(e) for e in range(NB)] * 2,
        out_specs=own,
    )
    return pl.pallas_call(
        attend_kernel,
        grid_spec=spec,
        out_shape=jax.ShapeDtypeStruct(query_tiles.shape, query_tiles.dtype),
        compiler_params=pltpu.CompilerParams(vmem_limit_bytes=48 * 1024 * 1024),
    )(local_lists, ext_counts, query_tiles, *([ext_keys] * NB), *([ext_values] * NB))


def shards(queries, keys, values, neighbors, tile_counts):
    block_queries, block_keys, block_values = (
        lax.all_to_all(queries, "head", split_axis=1, concat_axis=0, tiled=True),
        lax.all_to_all(keys, "head", split_axis=1, concat_axis=0, tiled=True),
        lax.all_to_all(values, "head", split_axis=1, concat_axis=0, tiled=True),
    )
    tiles_here = tile_counts.shape[0]
    local_width = block_queries.shape[1]
    local_heads = local_width // DH
    earlier = []
    later = []
    for distance in range(1, HOPS + 1):
        taken = min(tiles_here, REACH - (distance - 1) * tiles_here)
        rows_taken = taken * TILE
        sent_back = (block_keys[-rows_taken:], block_values[-rows_taken:], tile_counts[-taken:])
        earlier = [shifted((sent_back[0], sent_back[1], sent_back[2]), "ctx", distance)] + earlier
        sent_fore = (block_keys[:rows_taken], block_values[:rows_taken], tile_counts[:taken])
        later = later + [shifted((sent_fore[0], sent_fore[1], sent_fore[2]), "ctx", -distance)]
    before = join_pieces(earlier)
    after = join_pieces(later)
    ext_tiles = tiles_here + 2 * REACH
    ext_keys = jnp.concatenate([before[0], block_keys, after[0]], axis=0).reshape(
        ext_tiles, TILE, local_width
    )
    ext_values = jnp.concatenate([before[1], block_values, after[1]], axis=0).reshape(
        ext_tiles, TILE, local_width
    )
    ext_counts = jnp.concatenate([before[2], tile_counts, after[2]], axis=0)
    first_tile = lax.axis_index("ctx") * tiles_here - REACH
    local_lists = jnp.clip(neighbors - first_tile, 0, ext_tiles - 1).astype(jnp.int32)
    query_tiles = block_queries.reshape(tiles_here, TILE, local_width)
    outputs = attend(local_lists, ext_counts.astype(jnp.int32), query_tiles, ext_keys, ext_values)
    outputs = outputs.reshape(tiles_here * TILE, local_width)
    return lax.all_to_all(outputs, "head", split_axis=0, concat_axis=1, tiled=True)


def solution(mesh):
    placed = (
        P(("clips", "ctx", "head"), None),
        P(("clips", "ctx", "head"), None),
        P(("clips", "ctx", "head"), None),
        P(("clips", "ctx"), None),
        P(("clips", "ctx")),
    )
    return jax.shard_map(
        shards,
        mesh=mesh,
        in_specs=placed,
        out_specs=P(("clips", "ctx", "head"), None),
        check_vma=False,
    )
```

```python
import jax
import jax.numpy as jnp
from jax import lax
from jax.sharding import PartitionSpec as P
from jax.experimental import pallas as pl
from jax.experimental.pallas import tpu as pltpu

DH = 128
TILE = 384
NB = 8
REACH = 10
HOPS = 4


def shifted(array, axis, by):
    peers = lax.axis_size(axis)
    pairs = [(i, i + by) for i in range(peers) if 0 <= i + by < peers]
    return lax.ppermute(array, axis, pairs)


def attend_kernel(lists_ref, counts_ref, query_ref, *refs):
    key_refs = refs[:NB]
    value_refs = refs[NB : 2 * NB]
    out_ref = refs[2 * NB]
    tile = pl.program_id(0)
    query_rows = query_ref[...]
    slot_index = lax.broadcasted_iota(jnp.int32, (TILE, TILE), 1)
    scores = []
    for entry in range(NB):
        part = lax.dot_general(
            query_rows, key_refs[entry][...], (((1,), (1,)), ((), ())),
            preferred_element_type=jnp.float32,
        ) * DH ** (-0.5)
        live = slot_index < counts_ref[lists_ref[tile, entry]]
        scores.append(jnp.where(live, part, -jnp.inf))
    highest = scores[0].max(axis=1, keepdims=True)
    for part in scores[1:]:
        highest = jnp.maximum(highest, part.max(axis=1, keepdims=True))
    totals = jnp.zeros((TILE, 1), jnp.float32)
    summed = jnp.zeros((TILE, DH), jnp.float32)
    for entry in range(NB):
        weights = jnp.exp(scores[entry] - highest)
        totals = totals + weights.sum(axis=1, keepdims=True)
        summed = summed + jnp.dot(
            weights.astype(jnp.bfloat16), value_refs[entry][...],
            preferred_element_type=jnp.float32,
        )
    out_ref[...] = (summed / totals).astype(out_ref.dtype)


def attend(local_lists, ext_counts, query_tiles, ext_kv):
    tiles_here, _, local_width = query_tiles.shape
    local_heads = local_width // DH
    own = pl.BlockSpec((None, TILE, DH), lambda t, h, lists, counts: (t, 0, h))

    def listed(entry, offset):
        return pl.BlockSpec(
            (None, TILE, DH), lambda t, h, lists, counts: (lists[t, entry], 0, h + offset)
        )

    spec = pltpu.PrefetchScalarGridSpec(
        num_scalar_prefetch=2,
        grid=(tiles_here, local_heads),
        in_specs=[own] + [listed(e, 0) for e in range(NB)] + [listed(e, local_heads) for e in range(NB)],
        out_specs=own,
    )
    return pl.pallas_call(
        attend_kernel,
        grid_spec=spec,
        out_shape=jax.ShapeDtypeStruct(query_tiles.shape, query_tiles.dtype),
        compiler_params=pltpu.CompilerParams(vmem_limit_bytes=48 * 1024 * 1024),
    )(local_lists, ext_counts, query_tiles, *([ext_kv] * (2 * NB)))


def shards(queries, keys, values, neighbors, tile_counts):
    rows, width = queries.shape
    head_peers = lax.axis_size("head")
    group = width // head_peers
    stacked = jnp.stack([queries, keys, values], axis=1).reshape(rows, 3, head_peers, group)
    moved = lax.all_to_all(stacked, "head", split_axis=2, concat_axis=0, tiled=True)
    block_queries = moved[:, 0, 0]
    block_kv = moved[:, 1:, 0].reshape(rows * head_peers, 2 * group)
    tiles_here = tile_counts.shape[0]
    local_heads = group // DH
    ctx_peers = lax.axis_size("ctx")
    if ctx_peers <= 2 * HOPS + 1:
        ext_tiles = ctx_peers * tiles_here
        ext_kv = lax.all_gather(block_kv, "ctx", axis=0, tiled=True)
        ext_counts = lax.all_gather(tile_counts, "ctx", axis=0, tiled=True)
        first_tile = 0
    else:
        earlier = []
        later = []
        for distance in range(1, HOPS + 1):
            taken = min(tiles_here, REACH - (distance - 1) * tiles_here)
            rows_taken = taken * TILE
            earlier = [shifted((block_kv[-rows_taken:], tile_counts[-taken:]), "ctx", distance)] + earlier
            later = later + [shifted((block_kv[:rows_taken], tile_counts[:taken]), "ctx", -distance)]
        ext_tiles = tiles_here + 2 * REACH
        ext_kv = jnp.concatenate([p[0] for p in earlier] + [block_kv] + [p[0] for p in later], axis=0)
        ext_counts = jnp.concatenate([p[1] for p in earlier] + [tile_counts] + [p[1] for p in later], axis=0)
        first_tile = lax.axis_index("ctx") * tiles_here - REACH
    ext_kv = ext_kv.reshape(ext_tiles, TILE, 2 * group)
    local_lists = jnp.clip(neighbors - first_tile, 0, ext_tiles - 1).astype(jnp.int32)
    query_tiles = block_queries.reshape(tiles_here, TILE, group)
    outputs = attend(local_lists, ext_counts.astype(jnp.int32), query_tiles, ext_kv)
    outputs = outputs.reshape(tiles_here * TILE, group)
    return lax.all_to_all(outputs, "head", split_axis=0, concat_axis=1, tiled=True)


def solution(mesh):
    placed = (
        P(("clips", "ctx", "head"), None),
        P(("clips", "ctx", "head"), None),
        P(("clips", "ctx", "head"), None),
        P(("clips", "ctx"), None),
        P(("clips", "ctx")),
    )
    return jax.shard_map(
        shards,
        mesh=mesh,
        in_specs=placed,
        out_specs=P(("clips", "ctx", "head"), None),
        check_vma=False,
    )
```

```python
import jax
import jax.numpy as jnp
from jax import lax
from jax.sharding import PartitionSpec as P
from jax.experimental import pallas as pl
from jax.experimental.pallas import tpu as pltpu

DH = 128
TILE = 384
NB = 8
REACH = 10
HOPS = 4


def shifted(array, axis, by):
    peers = lax.axis_size(axis)
    pairs = [(i, i + by) for i in range(peers) if 0 <= i + by < peers]
    return lax.ppermute(array, axis, pairs)


def attend_kernel(lists_ref, counts_ref, query_ref, *refs):
    key_refs = refs[:NB]
    value_refs = refs[NB : 2 * NB]
    out_ref = refs[2 * NB]
    tile = pl.program_id(0)
    query_rows = query_ref[...]
    slot_index = lax.broadcasted_iota(jnp.int32, (TILE, TILE), 1)
    scores = []
    for entry in range(NB):
        part = lax.dot_general(
            query_rows, key_refs[entry][...], (((1,), (1,)), ((), ())),
            preferred_element_type=jnp.float32,
        ) * DH ** (-0.5)
        live = slot_index < counts_ref[lists_ref[tile, entry]]
        scores.append(jnp.where(live, part, -jnp.inf))
    highest = scores[0].max(axis=1, keepdims=True)
    for part in scores[1:]:
        highest = jnp.maximum(highest, part.max(axis=1, keepdims=True))
    totals = jnp.zeros((TILE, 1), jnp.float32)
    summed = jnp.zeros((TILE, DH), jnp.float32)
    for entry in range(NB):
        weights = jnp.exp(scores[entry] - highest)
        totals = totals + weights.sum(axis=1, keepdims=True)
        summed = summed + jnp.dot(
            weights.astype(jnp.bfloat16), value_refs[entry][...],
            preferred_element_type=jnp.float32,
        )
    out_ref[...] = (summed / totals).astype(out_ref.dtype)


def attend(local_lists, ext_counts, query_tiles, ext_kv):
    tiles_here, _, local_width = query_tiles.shape
    local_heads = local_width // DH
    own = pl.BlockSpec((None, TILE, DH), lambda t, h, lists, counts: (t, 0, h))

    def listed(entry, offset):
        return pl.BlockSpec(
            (None, TILE, DH), lambda t, h, lists, counts: (lists[t, entry], 0, h + offset)
        )

    spec = pltpu.PrefetchScalarGridSpec(
        num_scalar_prefetch=2,
        grid=(tiles_here, local_heads),
        in_specs=[own] + [listed(e, 0) for e in range(NB)] + [listed(e, local_heads) for e in range(NB)],
        out_specs=own,
    )
    return pl.pallas_call(
        attend_kernel,
        grid_spec=spec,
        out_shape=jax.ShapeDtypeStruct(query_tiles.shape, query_tiles.dtype),
        compiler_params=pltpu.CompilerParams(vmem_limit_bytes=48 * 1024 * 1024),
    )(local_lists, ext_counts, query_tiles, *([ext_kv] * (2 * NB)))


def shards(queries, keys, values, neighbors, tile_counts):
    rows, width = queries.shape
    head_peers = lax.axis_size("head")
    group = width // head_peers
    paired = jnp.concatenate(
        [keys.reshape(rows, head_peers, group), values.reshape(rows, head_peers, group)], axis=2
    )
    block_kv = lax.all_to_all(paired, "head", split_axis=1, concat_axis=0, tiled=True)
    block_kv = block_kv.reshape(rows * head_peers, 2 * group)
    tiles_here = tile_counts.shape[0]
    local_heads = group // DH
    ctx_peers = lax.axis_size("ctx")
    if ctx_peers <= 2 * HOPS + 1:
        ext_tiles = ctx_peers * tiles_here
        ext_kv = lax.all_gather(block_kv, "ctx", axis=0, tiled=True)
        ext_counts = lax.all_gather(tile_counts, "ctx", axis=0, tiled=True)
        first_tile = 0
    else:
        earlier = []
        later = []
        for distance in range(1, HOPS + 1):
            taken = min(tiles_here, REACH - (distance - 1) * tiles_here)
            rows_taken = taken * TILE
            earlier = [shifted((block_kv[-rows_taken:], tile_counts[-taken:]), "ctx", distance)] + earlier
            later = later + [shifted((block_kv[:rows_taken], tile_counts[:taken]), "ctx", -distance)]
        ext_tiles = tiles_here + 2 * REACH
        ext_kv = jnp.concatenate([p[0] for p in earlier] + [block_kv] + [p[0] for p in later], axis=0)
        ext_counts = jnp.concatenate([p[1] for p in earlier] + [tile_counts] + [p[1] for p in later], axis=0)
        first_tile = lax.axis_index("ctx") * tiles_here - REACH
    ext_kv = ext_kv.reshape(ext_tiles, TILE, 2 * group)
    local_lists = jnp.clip(neighbors - first_tile, 0, ext_tiles - 1).astype(jnp.int32)
    block_queries = lax.all_to_all(queries, "head", split_axis=1, concat_axis=0, tiled=True)
    query_tiles = block_queries.reshape(tiles_here, TILE, group)
    outputs = attend(local_lists, ext_counts.astype(jnp.int32), query_tiles, ext_kv)
    outputs = outputs.reshape(tiles_here * TILE, group)
    return lax.all_to_all(outputs, "head", split_axis=0, concat_axis=1, tiled=True)


def solution(mesh):
    placed = (
        P(("clips", "ctx", "head"), None),
        P(("clips", "ctx", "head"), None),
        P(("clips", "ctx", "head"), None),
        P(("clips", "ctx"), None),
        P(("clips", "ctx")),
    )
    return jax.shard_map(
        shards,
        mesh=mesh,
        in_specs=placed,
        out_specs=P(("clips", "ctx", "head"), None),
        check_vma=False,
    )
```

```python
import jax
import jax.numpy as jnp
from jax import lax
from jax.sharding import PartitionSpec as P
from jax.experimental import pallas as pl
from jax.experimental.pallas import tpu as pltpu

DH = 128
TILE = 384
NB = 8
REACH = 10
HOPS = 4


def shifted(array, axis, by):
    peers = lax.axis_size(axis)
    pairs = [(i, i + by) for i in range(peers) if 0 <= i + by < peers]
    return lax.ppermute(array, axis, pairs)


def attend_kernel(lists_ref, counts_ref, query_ref, *refs):
    key_refs = refs[:NB]
    value_refs = refs[NB : 2 * NB]
    out_ref = refs[2 * NB]
    tile = pl.program_id(0)
    query_rows = query_ref[...]
    slot_index = lax.broadcasted_iota(jnp.int32, (TILE, TILE), 1)
    scores = []
    for entry in range(NB):
        part = lax.dot_general(
            query_rows, key_refs[entry][...], (((1,), (1,)), ((), ())),
            preferred_element_type=jnp.float32,
        ) * DH ** (-0.5)
        live = slot_index < counts_ref[lists_ref[tile, entry]]
        scores.append(jnp.where(live, part, -jnp.inf))
    highest = scores[0].max(axis=1, keepdims=True)
    for part in scores[1:]:
        highest = jnp.maximum(highest, part.max(axis=1, keepdims=True))
    totals = jnp.zeros((TILE, 1), jnp.float32)
    summed = jnp.zeros((TILE, DH), jnp.float32)
    for entry in range(NB):
        weights = jnp.exp(scores[entry] - highest)
        totals = totals + weights.sum(axis=1, keepdims=True)
        summed = summed + jnp.dot(
            weights.astype(jnp.bfloat16), value_refs[entry][...],
            preferred_element_type=jnp.float32,
        )
    out_ref[...] = (summed / totals).astype(out_ref.dtype)


def attend(local_lists, ext_counts, query_tiles, ext_kv, head):
    tiles_here, _, local_width = query_tiles.shape
    local_heads = local_width // DH
    own = pl.BlockSpec((None, TILE, DH), lambda t, h, lists, counts: (t, 0, h + head))
    back = pl.BlockSpec((None, TILE, DH), lambda t, h, lists, counts: (t, 0, 0))

    def listed(entry, offset):
        return pl.BlockSpec(
            (None, TILE, DH),
            lambda t, h, lists, counts: (lists[t, entry], 0, h + head + offset),
        )

    spec = pltpu.PrefetchScalarGridSpec(
        num_scalar_prefetch=2,
        grid=(tiles_here, 1),
        in_specs=[own] + [listed(e, 0) for e in range(NB)] + [listed(e, local_heads) for e in range(NB)],
        out_specs=back,
    )
    return pl.pallas_call(
        attend_kernel,
        grid_spec=spec,
        out_shape=jax.ShapeDtypeStruct((tiles_here, TILE, DH), query_tiles.dtype),
        compiler_params=pltpu.CompilerParams(vmem_limit_bytes=48 * 1024 * 1024),
    )(local_lists, ext_counts, query_tiles, *([ext_kv] * (2 * NB)))


def shards(queries, keys, values, neighbors, tile_counts):
    rows, width = queries.shape
    head_peers = lax.axis_size("head")
    group = width // head_peers
    paired = jnp.concatenate(
        [keys.reshape(rows, head_peers, group), values.reshape(rows, head_peers, group)], axis=2
    )
    block_kv = lax.all_to_all(paired, "head", split_axis=1, concat_axis=0, tiled=True)
    block_kv = block_kv.reshape(rows * head_peers, 2 * group)
    tiles_here = tile_counts.shape[0]
    local_heads = group // DH
    ctx_peers = lax.axis_size("ctx")
    if ctx_peers <= 2 * HOPS + 1:
        ext_tiles = ctx_peers * tiles_here
        ext_kv = lax.all_gather(block_kv, "ctx", axis=0, tiled=True)
        ext_counts = lax.all_gather(tile_counts, "ctx", axis=0, tiled=True)
        first_tile = 0
    else:
        earlier = []
        later = []
        for distance in range(1, HOPS + 1):
            taken = min(tiles_here, REACH - (distance - 1) * tiles_here)
            rows_taken = taken * TILE
            earlier = [shifted((block_kv[-rows_taken:], tile_counts[-taken:]), "ctx", distance)] + earlier
            later = later + [shifted((block_kv[:rows_taken], tile_counts[:taken]), "ctx", -distance)]
        ext_tiles = tiles_here + 2 * REACH
        ext_kv = jnp.concatenate([p[0] for p in earlier] + [block_kv] + [p[0] for p in later], axis=0)
        ext_counts = jnp.concatenate([p[1] for p in earlier] + [tile_counts] + [p[1] for p in later], axis=0)
        first_tile = lax.axis_index("ctx") * tiles_here - REACH
    ext_kv = ext_kv.reshape(ext_tiles, TILE, 2 * group)
    local_lists = jnp.clip(neighbors - first_tile, 0, ext_tiles - 1).astype(jnp.int32)
    block_queries = lax.all_to_all(queries, "head", split_axis=1, concat_axis=0, tiled=True)
    query_tiles = block_queries.reshape(tiles_here, TILE, group)
    returned = []
    for head in range(local_heads):
        outputs = attend(local_lists, ext_counts.astype(jnp.int32), query_tiles, ext_kv, head)
        outputs = outputs.reshape(tiles_here * TILE, DH)
        returned.append(lax.all_to_all(outputs, "head", split_axis=0, concat_axis=1, tiled=True))
    joined = jnp.stack([piece.reshape(rows, head_peers, DH) for piece in returned], axis=2)
    return joined.reshape(rows, width)


def solution(mesh):
    placed = (
        P(("clips", "ctx", "head"), None),
        P(("clips", "ctx", "head"), None),
        P(("clips", "ctx", "head"), None),
        P(("clips", "ctx"), None),
        P(("clips", "ctx")),
    )
    return jax.shard_map(
        shards,
        mesh=mesh,
        in_specs=placed,
        out_specs=P(("clips", "ctx", "head"), None),
        check_vma=False,
    )
```

```python
import jax
import jax.numpy as jnp
from jax import lax
from jax.sharding import PartitionSpec as P
from jax.experimental import pallas as pl
from jax.experimental.pallas import tpu as pltpu

DH = 128
TILE = 384
NB = 8
REACH = 10
HOPS = 4


def shifted(array, axis, by):
    peers = lax.axis_size(axis)
    pairs = [(i, i + by) for i in range(peers) if 0 <= i + by < peers]
    return lax.ppermute(array, axis, pairs)


def attend_kernel(lists_ref, counts_ref, query_ref, *refs):
    key_refs = refs[:NB]
    value_refs = refs[NB : 2 * NB]
    out_ref = refs[2 * NB]
    tile = pl.program_id(0)
    query_rows = query_ref[...]
    slot_index = lax.broadcasted_iota(jnp.int32, (TILE, TILE), 1)
    scores = []
    for entry in range(NB):
        part = lax.dot_general(
            query_rows, key_refs[entry][...], (((1,), (1,)), ((), ())),
            preferred_element_type=jnp.float32,
        ) * DH ** (-0.5)
        live = slot_index < counts_ref[lists_ref[tile, entry]]
        scores.append(jnp.where(live, part, -jnp.inf))
    highest = scores[0].max(axis=1, keepdims=True)
    for part in scores[1:]:
        highest = jnp.maximum(highest, part.max(axis=1, keepdims=True))
    totals = jnp.zeros((TILE, 1), jnp.float32)
    summed = jnp.zeros((TILE, DH), jnp.float32)
    for entry in range(NB):
        weights = jnp.exp(scores[entry] - highest)
        totals = totals + weights.sum(axis=1, keepdims=True)
        summed = summed + jnp.dot(
            weights.astype(jnp.bfloat16), value_refs[entry][...],
            preferred_element_type=jnp.float32,
        )
    out_ref[...] = (summed / totals).astype(out_ref.dtype)


def attend(local_lists, ext_counts, query_tiles, ext_keys, ext_values):
    tiles_here, _, local_width = query_tiles.shape
    local_heads = local_width // DH
    own = pl.BlockSpec((None, TILE, DH), lambda t, h, lists, counts: (t, 0, h))

    def listed(entry, offset):
        return pl.BlockSpec(
            (None, TILE, DH), lambda t, h, lists, counts: (lists[t, entry], 0, h + offset)
        )

    spec = pltpu.PrefetchScalarGridSpec(
        num_scalar_prefetch=2,
        grid=(tiles_here, local_heads),
        in_specs=[own] + [listed(e, 0) for e in range(NB)] * 2,
        out_specs=own,
    )
    return pl.pallas_call(
        attend_kernel,
        grid_spec=spec,
        out_shape=jax.ShapeDtypeStruct(query_tiles.shape, query_tiles.dtype),
        compiler_params=pltpu.CompilerParams(vmem_limit_bytes=48 * 1024 * 1024),
    )(local_lists, ext_counts, query_tiles, *([ext_keys] * NB), *([ext_values] * NB))


def shards(queries, keys, values, neighbors, tile_counts):
    rows, width = queries.shape
    head_peers = lax.axis_size("head")
    group = width // head_peers
    block_keys = lax.all_to_all(keys, "head", split_axis=1, concat_axis=0, tiled=True)
    tiles_here = tile_counts.shape[0]
    local_heads = group // DH
    ctx_peers = lax.axis_size("ctx")
    if ctx_peers <= 2 * HOPS + 1:
        ext_tiles = ctx_peers * tiles_here
        ext_keys = lax.all_gather(block_keys, "ctx", axis=0, tiled=True)
        block_values = lax.all_to_all(values, "head", split_axis=1, concat_axis=0, tiled=True)
        ext_values = lax.all_gather(block_values, "ctx", axis=0, tiled=True)
        ext_counts = lax.all_gather(tile_counts, "ctx", axis=0, tiled=True)
        first_tile = 0
    else:
        block_values = lax.all_to_all(values, "head", split_axis=1, concat_axis=0, tiled=True)
        block_kv = jnp.concatenate([block_keys, block_values], axis=1)
        earlier = []
        later = []
        for distance in range(1, HOPS + 1):
            taken = min(tiles_here, REACH - (distance - 1) * tiles_here)
            rows_taken = taken * TILE
            earlier = [shifted((block_kv[-rows_taken:], tile_counts[-taken:]), "ctx", distance)] + earlier
            later = later + [shifted((block_kv[:rows_taken], tile_counts[:taken]), "ctx", -distance)]
        ext_tiles = tiles_here + 2 * REACH
        ext_kv = jnp.concatenate([p[0] for p in earlier] + [block_kv] + [p[0] for p in later], axis=0)
        ext_keys = ext_kv[:, :group]
        ext_values = ext_kv[:, group:]
        ext_counts = jnp.concatenate([p[1] for p in earlier] + [tile_counts] + [p[1] for p in later], axis=0)
        first_tile = lax.axis_index("ctx") * tiles_here - REACH
    ext_keys = ext_keys.reshape(ext_tiles, TILE, group)
    ext_values = ext_values.reshape(ext_tiles, TILE, group)
    local_lists = jnp.clip(neighbors - first_tile, 0, ext_tiles - 1).astype(jnp.int32)
    block_queries = lax.all_to_all(queries, "head", split_axis=1, concat_axis=0, tiled=True)
    query_tiles = block_queries.reshape(tiles_here, TILE, group)
    outputs = attend(local_lists, ext_counts.astype(jnp.int32), query_tiles, ext_keys, ext_values)
    outputs = outputs.reshape(tiles_here * TILE, group)
    return lax.all_to_all(outputs, "head", split_axis=0, concat_axis=1, tiled=True)


def solution(mesh):
    placed = (
        P(("clips", "ctx", "head"), None),
        P(("clips", "ctx", "head"), None),
        P(("clips", "ctx", "head"), None),
        P(("clips", "ctx"), None),
        P(("clips", "ctx")),
    )
    return jax.shard_map(
        shards,
        mesh=mesh,
        in_specs=placed,
        out_specs=P(("clips", "ctx", "head"), None),
        check_vma=False,
    )
```

```python
import jax
import jax.numpy as jnp
from jax import lax
from jax.sharding import PartitionSpec as P
from jax.experimental import pallas as pl
from jax.experimental.pallas import tpu as pltpu

DH = 128
TILE = 384
NB = 8
REACH = 10
HOPS = 4


def shifted(array, axis, by):
    peers = lax.axis_size(axis)
    pairs = [(i, i + by) for i in range(peers) if 0 <= i + by < peers]
    return lax.ppermute(array, axis, pairs)


def attend_kernel(lists_ref, counts_ref, query_ref, *refs):
    key_refs = refs[:NB]
    value_refs = refs[NB : 2 * NB]
    out_ref = refs[2 * NB]
    tile = pl.program_id(0)
    query_rows = query_ref[...]
    slot_index = lax.broadcasted_iota(jnp.int32, (1, TILE), 1)
    scores = []
    for entry in range(NB):
        part = lax.dot_general(
            query_rows, key_refs[entry][...], (((1,), (1,)), ((), ())),
            preferred_element_type=jnp.float32,
        ) * DH ** (-0.5)
        live = slot_index < counts_ref[lists_ref[tile, entry]]
        scores.append(jnp.where(live, part, -jnp.inf))
    highest = scores[0].max(axis=1, keepdims=True)
    for part in scores[1:]:
        highest = jnp.maximum(highest, part.max(axis=1, keepdims=True))
    totals = jnp.zeros((TILE, 1), jnp.float32)
    summed = jnp.zeros((TILE, DH), jnp.float32)
    for entry in range(NB):
        weights = jnp.exp(scores[entry] - highest)
        totals = totals + weights.sum(axis=1, keepdims=True)
        summed = summed + jnp.dot(
            weights.astype(jnp.bfloat16), value_refs[entry][...],
            preferred_element_type=jnp.float32,
        )
    out_ref[...] = (summed / totals).astype(out_ref.dtype)


def attend(local_lists, ext_counts, query_tiles, ext_kv):
    tiles_here, _, local_width = query_tiles.shape
    local_heads = local_width // DH
    own = pl.BlockSpec((None, TILE, DH), lambda t, h, lists, counts: (t, 0, h))

    def listed(entry, offset):
        return pl.BlockSpec(
            (None, TILE, DH), lambda t, h, lists, counts: (lists[t, entry], 0, h + offset)
        )

    spec = pltpu.PrefetchScalarGridSpec(
        num_scalar_prefetch=2,
        grid=(tiles_here, local_heads),
        in_specs=[own] + [listed(e, 0) for e in range(NB)] + [listed(e, local_heads) for e in range(NB)],
        out_specs=own,
    )
    return pl.pallas_call(
        attend_kernel,
        grid_spec=spec,
        out_shape=jax.ShapeDtypeStruct(query_tiles.shape, query_tiles.dtype),
        compiler_params=pltpu.CompilerParams(vmem_limit_bytes=48 * 1024 * 1024),
    )(local_lists, ext_counts, query_tiles, *([ext_kv] * (2 * NB)))


def shards(queries, keys, values, neighbors, tile_counts):
    rows, width = queries.shape
    head_peers = lax.axis_size("head")
    group = width // head_peers
    paired = jnp.concatenate(
        [keys.reshape(rows, head_peers, group), values.reshape(rows, head_peers, group)], axis=2
    )
    block_kv = lax.all_to_all(paired, "head", split_axis=1, concat_axis=0, tiled=True)
    block_kv = block_kv.reshape(rows * head_peers, 2 * group)
    tiles_here = tile_counts.shape[0]
    local_heads = group // DH
    ctx_peers = lax.axis_size("ctx")
    if ctx_peers <= 2 * HOPS + 1:
        ext_tiles = ctx_peers * tiles_here
        ext_kv = lax.all_gather(block_kv, "ctx", axis=0, tiled=True)
        ext_counts = lax.all_gather(tile_counts, "ctx", axis=0, tiled=True)
        first_tile = 0
    else:
        earlier = []
        later = []
        for distance in range(1, HOPS + 1):
            taken = min(tiles_here, REACH - (distance - 1) * tiles_here)
            rows_taken = taken * TILE
            earlier = [shifted((block_kv[-rows_taken:], tile_counts[-taken:]), "ctx", distance)] + earlier
            later = later + [shifted((block_kv[:rows_taken], tile_counts[:taken]), "ctx", -distance)]
        ext_tiles = tiles_here + 2 * REACH
        ext_kv = jnp.concatenate([p[0] for p in earlier] + [block_kv] + [p[0] for p in later], axis=0)
        ext_counts = jnp.concatenate([p[1] for p in earlier] + [tile_counts] + [p[1] for p in later], axis=0)
        first_tile = lax.axis_index("ctx") * tiles_here - REACH
    ext_kv = ext_kv.reshape(ext_tiles, TILE, 2 * group)
    local_lists = jnp.clip(neighbors - first_tile, 0, ext_tiles - 1).astype(jnp.int32)
    block_queries = lax.all_to_all(queries, "head", split_axis=1, concat_axis=0, tiled=True)
    query_tiles = block_queries.reshape(tiles_here, TILE, group)
    outputs = attend(local_lists, ext_counts.astype(jnp.int32), query_tiles, ext_kv)
    outputs = outputs.reshape(tiles_here * TILE, group)
    return lax.all_to_all(outputs, "head", split_axis=0, concat_axis=1, tiled=True)


def solution(mesh):
    placed = (
        P(("clips", "ctx", "head"), None),
        P(("clips", "ctx", "head"), None),
        P(("clips", "ctx", "head"), None),
        P(("clips", "ctx"), None),
        P(("clips", "ctx")),
    )
    return jax.shard_map(
        shards,
        mesh=mesh,
        in_specs=placed,
        out_specs=P(("clips", "ctx", "head"), None),
        check_vma=False,
    )
```

```python
import jax
import jax.numpy as jnp
from jax import lax
from jax.sharding import PartitionSpec as P
from jax.experimental import pallas as pl
from jax.experimental.pallas import tpu as pltpu

DH = 128
TILE = 384
NB = 8
REACH = 10
HOPS = 4


def shifted(array, axis, by):
    peers = lax.axis_size(axis)
    pairs = [(i, i + by) for i in range(peers) if 0 <= i + by < peers]
    return lax.ppermute(array, axis, pairs)


def attend_kernel(lists_ref, counts_ref, query_ref, *refs):
    key_refs = refs[:NB]
    value_refs = refs[NB : 2 * NB]
    out_ref = refs[2 * NB]
    tile = pl.program_id(0)
    query_rows = query_ref[...]
    slot_index = lax.broadcasted_iota(jnp.int32, (TILE, TILE), 1)
    scores = []
    for entry in range(NB):
        part = lax.dot_general(
            query_rows, key_refs[entry][...], (((1,), (1,)), ((), ())),
            preferred_element_type=jnp.float32,
        ) * DH ** (-0.5)
        live = slot_index < counts_ref[lists_ref[tile, entry]]
        scores.append(jnp.where(live, part, -jnp.inf))
    highest = scores[0].max(axis=1, keepdims=True)
    for part in scores[1:]:
        highest = jnp.maximum(highest, part.max(axis=1, keepdims=True))
    totals = jnp.zeros((TILE, 1), jnp.float32)
    summed = jnp.zeros((TILE, DH), jnp.float32)
    for entry in range(NB):
        weights = jnp.exp(scores[entry] - highest)
        totals = totals + weights.sum(axis=1, keepdims=True)
        summed = summed + jnp.dot(
            weights.astype(jnp.bfloat16), value_refs[entry][...],
            preferred_element_type=jnp.float32,
        )
    out_ref[...] = (summed / totals).astype(out_ref.dtype)


def attend(local_lists, ext_counts, query_tiles, ext_kv):
    tiles_here, _, local_width = query_tiles.shape
    local_heads = local_width // DH
    own = pl.BlockSpec((None, TILE, DH), lambda t, h, lists, counts: (t, 0, h))

    def listed(entry, offset):
        return pl.BlockSpec(
            (None, TILE, DH), lambda t, h, lists, counts: (lists[t, entry], 0, h + offset)
        )

    spec = pltpu.PrefetchScalarGridSpec(
        num_scalar_prefetch=2,
        grid=(tiles_here, local_heads),
        in_specs=[own] + [listed(e, 0) for e in range(NB)] + [listed(e, local_heads) for e in range(NB)],
        out_specs=own,
    )
    return pl.pallas_call(
        attend_kernel,
        grid_spec=spec,
        out_shape=jax.ShapeDtypeStruct(query_tiles.shape, query_tiles.dtype),
        compiler_params=pltpu.CompilerParams(vmem_limit_bytes=48 * 1024 * 1024),
    )(local_lists, ext_counts, query_tiles, *([ext_kv] * (2 * NB)))


def shards(queries, keys, values, neighbors, tile_counts):
    rows, width = queries.shape
    head_peers = lax.axis_size("head")
    group = width // head_peers
    paired = jnp.concatenate(
        [keys.reshape(rows, head_peers, group), values.reshape(rows, head_peers, group)], axis=2
    )
    block_kv = lax.all_to_all(paired, "head", split_axis=1, concat_axis=0, tiled=True)
    block_kv = block_kv.reshape(rows * head_peers, 2 * group)
    tiles_here = tile_counts.shape[0]
    local_heads = group // DH
    ctx_peers = lax.axis_size("ctx")
    if ctx_peers <= 2 * HOPS + 1:
        ext_tiles = ctx_peers * tiles_here
        pieces = jnp.stack([tile_counts // 16, tile_counts % 16], axis=1).astype(jnp.bfloat16)
        ext_kv, pieces = lax.all_gather((block_kv, pieces), "ctx", axis=0, tiled=True)
        pieces = pieces.astype(jnp.int32)
        ext_counts = pieces[:, 0] * 16 + pieces[:, 1]
        first_tile = 0
    else:
        earlier = []
        later = []
        for distance in range(1, HOPS + 1):
            taken = min(tiles_here, REACH - (distance - 1) * tiles_here)
            rows_taken = taken * TILE
            earlier = [shifted((block_kv[-rows_taken:], tile_counts[-taken:]), "ctx", distance)] + earlier
            later = later + [shifted((block_kv[:rows_taken], tile_counts[:taken]), "ctx", -distance)]
        ext_tiles = tiles_here + 2 * REACH
        ext_kv = jnp.concatenate([p[0] for p in earlier] + [block_kv] + [p[0] for p in later], axis=0)
        ext_counts = jnp.concatenate([p[1] for p in earlier] + [tile_counts] + [p[1] for p in later], axis=0)
        first_tile = lax.axis_index("ctx") * tiles_here - REACH
    ext_kv = ext_kv.reshape(ext_tiles, TILE, 2 * group)
    local_lists = jnp.clip(neighbors - first_tile, 0, ext_tiles - 1).astype(jnp.int32)
    block_queries = lax.all_to_all(queries, "head", split_axis=1, concat_axis=0, tiled=True)
    query_tiles = block_queries.reshape(tiles_here, TILE, group)
    outputs = attend(local_lists, ext_counts.astype(jnp.int32), query_tiles, ext_kv)
    outputs = outputs.reshape(tiles_here * TILE, group)
    return lax.all_to_all(outputs, "head", split_axis=0, concat_axis=1, tiled=True)


def solution(mesh):
    placed = (
        P(("clips", "ctx", "head"), None),
        P(("clips", "ctx", "head"), None),
        P(("clips", "ctx", "head"), None),
        P(("clips", "ctx"), None),
        P(("clips", "ctx")),
    )
    return jax.shard_map(
        shards,
        mesh=mesh,
        in_specs=placed,
        out_specs=P(("clips", "ctx", "head"), None),
        check_vma=False,
    )
```
